32 devices in a mesh: dp: 8 (over z, x), seq: 4 (over y, core).
Axes of the slice: x: 2, y: 2, z: 4, core: 2. Of those that a mesh axis runs over, the one named last changes fastest.
Arguments:
- tokens: bfloat16 [32, 6144], P('dp', 'seq'), may hold values from -6 to 6
- expert_ids: int32 [32, 2], P('dp'), may hold values from 0 to 7, all different within a row; in each aligned block of 4 rows (0 to 3, 4 to 7, ...) at most 2 rows name the same one
- router: bfloat16 [6144, 8], P('seq'), may hold values from -0.21875 to 0.21875
- w_gate: bfloat16 [5, 6144, 16384], P(None, 'seq', 'dp'), may hold values from -0.078125 to 0.078125
- w_up: bfloat16 [5, 6144, 16384], P(None, 'seq', 'dp'), may hold values from -0.078125 to 0.078125
- w_down: bfloat16 [5, 16384, 6144], P(None, 'dp', 'seq'), may hold values from -0.046875 to 0.046875
Outputs:
- mixed: bfloat16 [32, 6144], P('dp', 'seq')
The draws below stay inside these ranges and needn't reach their ends.
Inputs may be any that keep to these rules, and one draw needn't show every extreme that they name: `expert_ids`: each row names 2 different experts. The 4 tokens of one index of dp name any expert at most 2 times, a bound that some block reaches.
All inputs are finite; a program needn't handle non-finite values.
Results may differ from the reference program's by a relative error of at most 0.0049.
Values may be sent and summed in bfloat16 or wider, within the bound.
No kernel may reach another device: no remote copies, remote signals or barrier semaphores. Data moves between devices by JAX's collectives and lax.ppermute only.
A program may use at most 192 MiB of HBM per device.

```python
import math
import jax
import jax.numpy as jnp
import numpy as np

D = 6144
FF = 16384
EXPERTS = 8
TOP = 2
WINDOW = 5
TOK_DEV = 4
MOST = 2
TOKENS = 32
N_DP = 8


def block_levels(rng, shape, pieces, smallest, largest):
    factor_of, own = 1.0, jax.random.fold_in(rng, 6)
    for dim, parts in pieces:
        steps = jnp.exp(jax.random.uniform(jax.random.fold_in(own, dim), (parts,), jnp.float32, smallest / len(pieces), largest / len(pieces)))
        factor_of = factor_of * jnp.repeat(steps, shape[dim] // parts).reshape([-1 if axis == dim else 1 for axis in range(len(shape))])
    return factor_of


def deal_out(own_key, own, number, rows, amount, top, most, skew):
    order = jax.random.permutation(own_key, amount)
    crowded, ordinary = shares(amount, rows * top, most, skew, True), shares(amount, rows * top, most, skew, False)
    places = jnp.arange(amount)

    def named(sizes, rotation):
        used = int((sizes > 0).sum())
        fixed = max(1, used // 4)
        passed = fixed + (places - fixed + rotation * (used - fixed)) % max(1, amount - fixed)
        return jnp.zeros((amount,), jnp.int32).at[order[jnp.where(places < fixed, places, passed)]].set(jnp.asarray(sizes, jnp.int32))

    sizes = jnp.where(number % 4 == 0, named(crowded, number // 4), named(ordinary, number - number // 4 - 1))
    mixed = jax.random.permutation(jax.random.fold_in(own, 3), amount)
    giver, sink = mixed[0:amount // 2 * 2:2], mixed[1:amount // 2 * 2:2]
    room = jnp.minimum(sizes[giver] - 1, most - sizes[sink]) // 2
    room = jnp.where((giver == order[0]) | (sink == order[0]) | (sizes[sink] == 0), 0, jnp.maximum(room, 0))
    passed = jax.random.randint(jax.random.fold_in(own, 4), (amount // 2,), 0, 1 << 20) % (room + 1)
    sizes = sizes.at[giver].add(-passed).at[sink].add(passed)
    labels = jnp.searchsorted(jnp.cumsum(sizes), jnp.arange(rows * top), side="right").astype(jnp.int32)
    listing = labels.reshape(top, rows).T
    listing = listing[jax.random.permutation(jax.random.fold_in(own, 1), rows)]
    rotation = jax.random.randint(jax.random.fold_in(own, 2), (rows, 1), 0, top)
    return jnp.take_along_axis(listing, (jnp.arange(top)[None, :] + rotation) % top, axis=1)


def shares(amount, total, reach, lean, full):
    weights = [(1 << 20) // math.isqrt(rank ** lean) + 1 for rank in range(1, amount + 1)]
    largest = reach if full else min(reach, max(-(-total // amount), total * weights[0] // sum(weights)))
    least = 1 if total - largest >= amount - 1 else 0
    given, surplus = [largest] + [least] * (amount - 1), total - largest - least * (amount - 1)
    while surplus > 0:
        candidates = [i for i in range(1, amount) if given[i] < largest] or [i for i in range(1, amount) if given[i] < reach]
        whole, left = sum([weights[i] for i in candidates]), surplus
        for i in candidates:
            extra = min(reach - given[i], max(1, left * weights[i] // whole), surplus)
            given[i] = given[i] + extra
            surplus = surplus - extra
    return np.array(given)


def scatter_about(rng, dims, deviation, bound, shards=(), held_as=jnp.bfloat16):
    factor_of = block_levels(rng, dims, shards, -0.22, 0.18) if shards else 1.0
    drawn = jax.random.normal(rng, dims, jnp.float32) * deviation * factor_of
    return jnp.minimum(jnp.maximum(drawn, -bound), bound).astype(held_as)


def setup_inputs(seed: int = 0) -> dict:
    key_list = jax.random.split(jax.random.key(seed), 7)
    tokens = scatter_about(key_list[0], (TOKENS, D), 1.0, 6.0, ((0, 8), (1, 4)))
    expert_ids_keys = jax.random.split(jax.random.fold_in(key_list[1], 1), TOKENS // TOK_DEV)
    expert_ids_turns = jax.random.permutation(jax.random.fold_in(key_list[1], 3), TOKENS // TOK_DEV)
    expert_ids = jax.vmap(lambda own, number: deal_out(jax.random.fold_in(key_list[1], 2), own, number, TOK_DEV, EXPERTS, TOP, MOST, 2))(expert_ids_keys, expert_ids_turns).reshape((TOKENS, TOP))
    router = scatter_about(key_list[2], (D, EXPERTS), (D // 9) ** -0.5, 0.21875, ((0, 4),))
    w_gate = scatter_about(key_list[3], (WINDOW, D, FF), D ** -0.5, 0.078125, ((1, 4), (2, 8)))
    w_up = scatter_about(key_list[4], (WINDOW, D, FF), D ** -0.5, 0.078125, ((1, 4), (2, 8)))
    w_down = scatter_about(key_list[5], (WINDOW, FF, D), FF ** -0.5, 0.046875, ((1, 8), (2, 4)))
    return {"tokens": tokens, "expert_ids": expert_ids, "router": router, "w_gate": w_gate, "w_up": w_up, "w_down": w_down}


def expert_rows(expert_ids, expert, capacity):
    member = jnp.any(expert_ids == expert, axis=1)
    position = jnp.cumsum(member.astype(jnp.int32)) - 1
    target = jnp.where(member, position, capacity).astype(jnp.int32)
    count_all = expert_ids.shape[0]
    row_token = jnp.zeros((capacity,), jnp.int32).at[target].set(jnp.arange(count_all, dtype=jnp.int32), mode="drop")
    return row_token, jnp.maximum(position, 0).astype(jnp.int32)


def reference(tokens, expert_ids, router, w_gate, w_up, w_down):
    capacity = MOST * N_DP
    logits = jnp.dot(tokens, router, preferred_element_type=jnp.float32)
    chosen = jnp.take_along_axis(logits, expert_ids, axis=1)
    share_first = 1.0 / (1.0 + jnp.exp(chosen[:, 1] - chosen[:, 0]))
    share_second = 1.0 / (1.0 + jnp.exp(chosen[:, 0] - chosen[:, 1]))
    totals = jnp.zeros(tokens.shape, jnp.float32)
    for expert in range(WINDOW):
        row_token, position = expert_rows(expert_ids, expert, capacity)
        buffer = tokens[row_token]
        gate_part = jnp.dot(buffer, w_gate[expert], preferred_element_type=jnp.float32)
        up_part = jnp.dot(buffer, w_up[expert], preferred_element_type=jnp.float32)
        hidden = (jax.nn.silu(gate_part) * up_part).astype(jnp.bfloat16)
        expert_out = jnp.dot(hidden, w_down[expert], preferred_element_type=jnp.float32)
        weighting = jnp.where(expert_ids[:, 0] == expert, share_first, jnp.float32(0.0))
        weighting = weighting + jnp.where(expert_ids[:, 1] == expert, share_second, jnp.float32(0.0))
        totals = totals + weighting[:, None] * expert_out[position]
    return totals.astype(jnp.bfloat16)
```

```python
import functools

import jax
import jax.numpy as jnp
from jax import lax
from jax.experimental import pallas as pl
from jax.experimental.pallas import tpu as pltpu
from jax.sharding import PartitionSpec as P


LANES = 128
VMEM = pl.BlockSpec(memory_space=pltpu.VMEM)
HBM = pl.BlockSpec(memory_space=pltpu.HBM)


def swap(value, axis, bit):
    count = lax.axis_size(axis)
    return lax.ppermute(value, axis, [(i, i ^ bit) for i in range(count)])


def half_of(mine):
    core = lax.rem(lax.axis_index("seq"), 2)
    return core if mine else 1 - core


def gate_up_kernel(mine, ahead, x_ref, gate_hbm, up_hbm, out_ref, buffer, sems):
    experts, width, columns = gate_hbm.shape
    half = columns // 2
    start = pl.multiple_of(half_of(mine) * half, half)
    x = x_ref[:, :width]
    first = x_ref[:, width : width + 1].astype(jnp.float32)
    second = x_ref[:, width + 1 : width + 2].astype(jnp.float32)

    def copy(e, kind, slot):
        source = gate_hbm if kind == 0 else up_hbm
        return pltpu.make_async_copy(
            source.at[e, :, pl.ds(start, half)], buffer.at[slot, kind], sems.at[slot, kind]
        )

    for e in range(ahead):
        for kind in range(2):
            copy(e, kind, e).start()
    out_ref[...] = jnp.zeros_like(out_ref)

    @pl.loop(0, experts)
    def _(e):
        slot = lax.rem(e, ahead + 1)
        number = lax.convert_element_type(e, jnp.float32)
        for kind in range(2):
            copy(e, kind, slot).wait()

            @pl.when(e + ahead < experts)
            def _():
                copy(e + ahead, kind, lax.rem(e + ahead, ahead + 1)).start()

            value = jnp.dot(x, buffer[slot, kind], preferred_element_type=jnp.float32)
            for k, named in ((0, first), (1, second)):
                old = out_ref[kind, k].astype(jnp.float32)
                out_ref[kind, k] = jnp.where(named == number, value, old).astype(out_ref.dtype)


def gate_up(mine, x, w_gate, w_up, dtype):
    experts, width, columns = w_gate.shape
    rows, half = x.shape[0], columns // 2
    ahead = min(3, experts)
    return pl.pallas_call(
        functools.partial(gate_up_kernel, mine, ahead),
        out_shape=jax.ShapeDtypeStruct((2, 2, rows, half), dtype),
        in_specs=[VMEM, HBM, HBM],
        out_specs=VMEM,
        scratch_shapes=[
            pltpu.VMEM((ahead + 1, 2, width, half), w_up.dtype),
            pltpu.SemaphoreType.DMA((ahead + 1, 2)),
        ],
        compiler_params=pltpu.CompilerParams(vmem_limit_bytes=40 << 20),
        cost_estimate=pl.CostEstimate(
            flops=2 * rows * experts * width * columns,
            bytes_accessed=2 * experts * width * columns,
            transcendentals=0,
        ),
        name="gate_up_mine" if mine else "gate_up_other",
    )(x, w_gate, w_up)


def hidden_kernel(pair_ref, far_ref, out_ref):
    gate = pair_ref[0] + far_ref[0].astype(jnp.float32)
    up = pair_ref[1] + far_ref[1].astype(jnp.float32)
    out_ref[...] = (gate / (1.0 + jnp.exp(-gate)) * up).astype(out_ref.dtype)


def hidden_of(pair, far):
    return pl.pallas_call(
        hidden_kernel,
        out_shape=jax.ShapeDtypeStruct(pair.shape[1:], far.dtype),
        in_specs=[VMEM, VMEM],
        out_specs=VMEM,
        compiler_params=pltpu.CompilerParams(vmem_limit_bytes=6 << 20),
        cost_estimate=pl.CostEstimate(
            flops=8 * pair.size, bytes_accessed=6 * pair.size, transcendentals=pair.size // 2
        ),
        name="silu_times_up",
    )(pair, far)


def load_kernel(source, gate_ref, out_ref, sems):
    del gate_ref
    copies = [
        pltpu.make_async_copy(source.at[e], out_ref.at[e], sems.at[e])
        for e in range(out_ref.shape[0])
    ]
    for copy in copies:
        copy.start()
    for copy in copies:
        copy.wait()


def load(source, after):
    held = pl.pallas_call(
        load_kernel,
        out_shape=pltpu.VMEM(source.shape, source.dtype),
        in_specs=[HBM, HBM],
        out_specs=VMEM,
        scratch_shapes=[pltpu.SemaphoreType.DMA((source.shape[0],))],
        compiler_params=pltpu.CompilerParams(vmem_limit_bytes=1 << 20),
        cost_estimate=pl.CostEstimate(
            flops=0, bytes_accessed=source.size * source.dtype.itemsize, transcendentals=0
        ),
    )(source, after)
    return held


def down_kernel(mine, last, x_ref, near_ref, far_ref, hidden_ref, down_ref, *rest):
    if last:
        before_ref, keep_ref, send_ref, total_ref = rest
    else:
        (total_ref,) = rest
    experts, columns, width = down_ref.shape
    half = columns // 2
    start = pl.multiple_of(half_of(mine) * half, half)
    rows = x_ref.shape[0]
    first = x_ref[:, width : width + 1].astype(jnp.float32)
    second = x_ref[:, width + 1 : width + 2].astype(jnp.float32)
    logits = near_ref[...] + far_ref[...]
    number = lax.broadcasted_iota(jnp.int32, logits.shape, 1).astype(jnp.float32)
    a = jnp.sum(jnp.where(number == first, logits, 0.0), axis=1, keepdims=True)
    b = jnp.sum(jnp.where(number == second, logits, 0.0), axis=1, keepdims=True)
    share_first = 1.0 / (1.0 + jnp.exp(b - a))
    share_second = 1.0 / (1.0 + jnp.exp(a - b))
    total_ref[...] = before_ref[...] if last else jnp.zeros_like(total_ref)
    h_first = hidden_ref[0].astype(jnp.float32)
    h_second = hidden_ref[1].astype(jnp.float32)

    @pl.loop(0, experts)
    def _(e):
        this = lax.convert_element_type(e, jnp.float32)
        in_first, in_second = first == this, second == this
        h = jnp.where(in_first, h_first, jnp.where(in_second, h_second, 0.0))
        weight = jnp.where(in_first, share_first, jnp.where(in_second, share_second, 0.0))
        out = jnp.dot(
            h.astype(jnp.bfloat16),
            down_ref[e, pl.ds(start, half), :],
            preferred_element_type=jnp.float32,
        )
        total_ref[...] += weight * out

    if last:
        keep_ref[...] = total_ref[: rows // 2]
        send_ref[...] = total_ref[rows // 2 :].astype(send_ref.dtype)


def down(mine, x, near, far, hidden, w_down, before=None):
    experts, columns, width = w_down.shape
    rows = x.shape[0]
    last = before is not None
    operands = [x, near, far, hidden, w_down] + ([before] if last else [])
    if last:
        out_shape = (
            jax.ShapeDtypeStruct((rows // 2, width), jnp.float32),
            jax.ShapeDtypeStruct((rows // 2, width), jnp.float32),
        )
        scratch = [pltpu.VMEM((rows, width), jnp.float32)]
    else:
        out_shape = jax.ShapeDtypeStruct((rows, width), jnp.float32)
        scratch = []
    return pl.pallas_call(
        functools.partial(down_kernel, mine, last),
        out_shape=out_shape,
        in_specs=[VMEM] * len(operands),
        out_specs=(VMEM, VMEM) if last else VMEM,
        scratch_shapes=scratch,
        compiler_params=pltpu.CompilerParams(vmem_limit_bytes=12 << 20),
        cost_estimate=pl.CostEstimate(
            flops=rows * experts * width * columns,
            bytes_accessed=experts * width * columns,
            transcendentals=0,
        ),
        name="down_last" if last else "down_mine",
    )(*operands)


def body(tokens, expert_ids, router, w_gate, w_up, w_down):
    bits = [1 << i for i in range((lax.axis_size("dp") - 1).bit_length())]
    local, width = tokens.shape
    named = jnp.pad(expert_ids.astype(tokens.dtype), ((0, 0), (0, LANES - expert_ids.shape[1])))
    x = lax.optimization_barrier(jnp.concatenate([tokens, named], axis=1))
    for bit in reversed(bits):
        x = jnp.concatenate([x, swap(x, "dp", bit)], axis=0)
        x = lax.optimization_barrier(x)
    logits = jnp.dot(x[:, :width], router, preferred_element_type=jnp.float32)
    logits = logits + swap(logits, "seq", 1)
    other = gate_up(False, x, w_gate, w_up, jnp.float32)
    arrived = swap(other, "seq", 1)
    mine = gate_up(True, x, w_gate, w_up, jnp.float32)
    pair = mine + arrived
    sent = pair.astype(jnp.bfloat16)
    down_fast = load(w_down, sent)
    far_logits = swap(logits, "seq", 2)
    hidden = hidden_of(pair, swap(sent, "seq", 2))
    hidden_other = swap(hidden, "seq", 1)
    part = down(True, x, logits, far_logits, hidden, down_fast)
    total, send = down(False, x, logits, far_logits, hidden_other, down_fast, part)
    for bit in bits:
        total = total + swap(send, "dp", bit)
        if total.shape[0] > local:
            rows = total.shape[0] // 2
            total, send = total[:rows], total[rows:]
    return total.astype(jnp.bfloat16)


def solution(mesh):
    placed = (
        P("dp", "seq"),
        P("dp", None),
        P("seq", None),
        P(None, "seq", "dp"),
        P(None, "seq", "dp"),
        P(None, "dp", "seq"),
    )
    return jax.shard_map(
        body, mesh=mesh, in_specs=placed, out_specs=P("dp", "seq"), check_vma=False
    )
```

```python
import functools

import jax
import jax.numpy as jnp
from jax import lax
from jax.experimental import pallas as pl
from jax.experimental.pallas import tpu as pltpu
from jax.sharding import PartitionSpec as P


LANES = 128
MIB = 1 << 20
WINDOWS = 3
AHEAD = 2
SLOTS = 8
VMEM = pl.BlockSpec(memory_space=pltpu.VMEM)
SMEM = pl.BlockSpec(memory_space=pltpu.SMEM)
HBM = pl.BlockSpec(memory_space=pltpu.HBM)


def steps_of(count):
    return [1 << i for i in range((count - 1).bit_length())]


def swap(value, axis, bit):
    count = lax.axis_size(axis)
    return lax.ppermute(value, axis, [(i, i ^ bit) for i in range(count)])


def cost(flops, moved):
    return pl.CostEstimate(flops=flops, bytes_accessed=moved, transcendentals=0)


def pack_kernel(token_hbm, id_hbm, out_ref, id_ref, sems):
    rows, width = token_hbm.shape
    token_copy = pltpu.make_async_copy(token_hbm, out_ref.at[:, pl.ds(0, width)], sems.at[0])
    id_copy = pltpu.make_async_copy(id_hbm, id_ref, sems.at[1])
    id_copy.start()
    token_copy.start()
    id_copy.wait()
    row = lax.broadcasted_iota(jnp.int32, (rows, rows), 0)
    lane = lax.broadcasted_iota(jnp.int32, (rows, rows), 1)
    place = lax.broadcasted_iota(jnp.int32, (rows, LANES), 1)
    named = jnp.zeros((rows, LANES), jnp.float32)
    for k in range(id_ref.shape[0]):
        numbers = jnp.broadcast_to(id_ref[k : k + 1, :].astype(jnp.float32), (rows, rows))
        column = jnp.sum(jnp.where(row == lane, numbers, 0.0), axis=1, keepdims=True)
        named = jnp.where(place == k, column, named)
    out_ref[:, width:] = named.astype(out_ref.dtype)
    token_copy.wait()


def pack(tokens, expert_ids):
    rows, width = tokens.shape
    return pl.pallas_call(
        pack_kernel,
        out_shape=jax.ShapeDtypeStruct((rows, width + LANES), tokens.dtype),
        in_specs=[HBM, HBM],
        out_specs=VMEM,
        scratch_shapes=[
            pltpu.VMEM(expert_ids.shape[::-1], expert_ids.dtype),
            pltpu.SemaphoreType.DMA((2,)),
        ],
        compiler_params=pltpu.CompilerParams(vmem_limit_bytes=MIB),
        name="pack",
    )(
        pltpu.with_memory_space_constraint(tokens, pltpu.HBM),
        pltpu.with_memory_space_constraint(expert_ids.T, pltpu.HBM),
    )


def block_copy(gate_hbm, up_hbm, number, kind, ring, sems):
    total, half = 2 * gate_hbm.shape[0], gate_hbm.shape[2] // 2
    core = lax.rem(lax.axis_index("seq"), 2)
    if isinstance(number, int):
        side, place, slot = number // total, number % total, number % ring.shape[0]
    else:
        side, place, slot = number // total, lax.rem(number, total), lax.rem(number, ring.shape[0])
    start = pl.multiple_of((core + 1 - side) % 2 * half, half)
    source = gate_hbm if kind == 0 else up_hbm
    return pltpu.make_async_copy(
        source.at[place // 2, :, pl.ds(start, half)], ring.at[slot], sems.at[slot]
    )


def start_block(gate_hbm, up_hbm, number, ring, sems):
    if isinstance(number, int):
        block_copy(gate_hbm, up_hbm, number, number % 2, ring, sems).start()
        return
    for kind in range(2):

        @pl.when(lax.rem(number, 2) == kind)
        def _():
            block_copy(gate_hbm, up_hbm, number, kind, ring, sems).start()


def load_first_kernel(number, gate_hbm, up_hbm, *refs):
    ring, sems = refs[-2:]
    start_block(gate_hbm, up_hbm, number, ring, sems)
    block_copy(gate_hbm, up_hbm, number, 0, ring, sems).wait()


def load_first(number, w_gate, w_up, ring):
    width, half = w_gate.shape[1], w_gate.shape[2] // 2
    slots = min(SLOTS, 2 * w_gate.shape[0])
    return pl.pallas_call(
        functools.partial(load_first_kernel, number),
        out_shape=pltpu.VMEM((slots, width, half), w_gate.dtype),
        in_specs=[HBM, HBM] + ([] if ring is None else [VMEM]),
        out_specs=VMEM,
        input_output_aliases={} if ring is None else {2: 0},
        scratch_shapes=[pltpu.SemaphoreType.DMA((slots,))],
        compiler_params=pltpu.CompilerParams(vmem_limit_bytes=MIB),
        cost_estimate=cost(0, 2 * width * half),
    )(w_gate, w_up, *([] if ring is None else [ring]))


def gate_up_kernel(begin, held, ahead, x_ref, gate_hbm, up_hbm, *refs):
    out_ref, ring, sems = refs[-3:]
    experts, width, _ = gate_hbm.shape
    total, slots = 2 * experts, ring.shape[0]
    stop = begin + total + ahead
    x = x_ref[:, :width]
    first = x_ref[:, width : width + 1].astype(jnp.float32)
    second = x_ref[:, width + 1 : width + 2].astype(jnp.float32)
    for number in range(begin + held, min(begin + slots - 1, stop)):
        start_block(gate_hbm, up_hbm, number, ring, sems)
    out_ref[...] = jnp.zeros_like(out_ref)

    @pl.loop(begin, begin + total)
    def _(number):
        @pl.when(number >= begin + held)
        def _():
            block_copy(gate_hbm, up_hbm, number, 0, ring, sems).wait()

        later = number + slots - 1

        @pl.when(later < stop)
        def _():
            start_block(gate_hbm, up_hbm, later, ring, sems)

        weights = ring[lax.rem(number, slots)]
        value = jnp.dot(x, weights, preferred_element_type=jnp.float32)
        kind, this = lax.rem(number, 2), ((number - begin) // 2).astype(jnp.float32)
        for k, named in ((0, first), (1, second)):
            out_ref[kind, k] = jnp.where(named == this, value, out_ref[kind, k])

    for number in range(begin + total, stop):
        block_copy(gate_hbm, up_hbm, number, 0, ring, sems).wait()


def gate_up(mine, x, w_gate, w_up, ring, held, ahead):
    experts, width, columns = w_gate.shape
    rows, half = x.shape[0], columns // 2
    slots = ring.shape[0]
    assert held < slots and ahead < slots
    return pl.pallas_call(
        functools.partial(gate_up_kernel, 2 * experts if mine else 0, held, ahead),
        out_shape=(
            jax.ShapeDtypeStruct((2, 2, rows, half), jnp.float32),
            pltpu.VMEM(ring.shape, ring.dtype),
        ),
        in_specs=[VMEM, HBM, HBM, VMEM],
        out_specs=(VMEM, VMEM),
        input_output_aliases={3: 1},
        scratch_shapes=[pltpu.SemaphoreType.DMA((slots,))],
        compiler_params=pltpu.CompilerParams(vmem_limit_bytes=4 * MIB),
        cost_estimate=cost(
            4 * rows * experts * width * half, 2 * (2 * experts - held + ahead) * width * half
        ),
        name="gate_up_mine" if mine else "gate_up_other",
    )(x, w_gate, w_up, ring)


def hidden_kernel(pair_ref, far_ref, out_ref):
    gate = pair_ref[0] + far_ref[0].astype(jnp.float32)
    up = pair_ref[1] + far_ref[1].astype(jnp.float32)
    out_ref[...] = (gate / (1.0 + jnp.exp(-gate)) * up).astype(out_ref.dtype)


def hidden_of(pair, far):
    return pl.pallas_call(
        hidden_kernel,
        out_shape=jax.ShapeDtypeStruct(pair.shape[1:], far.dtype),
        in_specs=[VMEM, VMEM],
        out_specs=VMEM,
        compiler_params=pltpu.CompilerParams(vmem_limit_bytes=6 * MIB),
        cost_estimate=pl.CostEstimate(
            flops=8 * pair.size, bytes_accessed=6 * pair.size, transcendentals=pair.size // 2
        ),
        name="silu_times_up",
    )(pair, far)


def piece_copy(mine, down_hbm, expert, held, sem):
    half = down_hbm.shape[1] // 2
    core = lax.rem(lax.axis_index("seq"), 2)
    start = pl.multiple_of((core if mine else 1 - core) * half, half)
    return pltpu.make_async_copy(down_hbm.at[expert, pl.ds(start, half), :], held.at[expert], sem)


def load_down_kernel(count, down_hbm, mine_ref, other_ref, sems):
    experts = down_hbm.shape[0]
    copies = [piece_copy(True, down_hbm, e, mine_ref, sems.at[e]) for e in range(experts)]
    for e in range(count):
        copies.append(piece_copy(False, down_hbm, e, other_ref, sems.at[experts + e]))
    for copy in copies:
        copy.start()
    for copy in copies:
        copy.wait()


def load_down(w_down, count):
    experts, half, width = w_down.shape[0], w_down.shape[1] // 2, w_down.shape[2]
    side = pltpu.VMEM((experts, half, width), w_down.dtype)
    return pl.pallas_call(
        functools.partial(load_down_kernel, count),
        out_shape=(side, side),
        in_specs=[HBM],
        out_specs=(VMEM, VMEM),
        scratch_shapes=[pltpu.SemaphoreType.DMA((2 * experts,))],
        compiler_params=pltpu.CompilerParams(vmem_limit_bytes=MIB),
        cost_estimate=cost(0, 2 * (experts + count) * half * width),
        name="load_down",
    )(w_down)


def down_kernel(last, begin, count, x_ref, near_ref, far_ref, hidden_ref, down_hbm, *refs):
    if last:
        _, before_ref, keep_ref, send_ref, other_ref, total_ref, sems = refs
        held = other_ref
    else:
        held, _, total_ref, other_ref, sems = refs
    copies = [
        piece_copy(False, down_hbm, begin + i, other_ref, sems.at[i]) for i in range(count)
    ]
    for copy in copies:
        copy.start()
    experts, _, width = down_hbm.shape
    rows = x_ref.shape[0]
    first = x_ref[:, width : width + 1].astype(jnp.float32)
    second = x_ref[:, width + 1 : width + 2].astype(jnp.float32)
    logits = near_ref[...] + far_ref[...]
    number = lax.broadcasted_iota(jnp.int32, logits.shape, 1).astype(jnp.float32)
    a = jnp.sum(jnp.where(number == first, logits, 0.0), axis=1, keepdims=True)
    b = jnp.sum(jnp.where(number == second, logits, 0.0), axis=1, keepdims=True)
    share_first = 1.0 / (1.0 + jnp.exp(b - a))
    share_second = 1.0 / (1.0 + jnp.exp(a - b))
    total_ref[...] = before_ref[...] if last else jnp.zeros_like(total_ref)
    h_first = hidden_ref[0].astype(jnp.float32)
    h_second = hidden_ref[1].astype(jnp.float32)

    @pl.loop(0, experts)
    def _(e):
        if last:
            for i in range(count):
                pl.when(e == begin + i)(copies[i].wait)
        this = e.astype(jnp.float32)
        in_first, in_second = first == this, second == this
        h = jnp.where(in_first, h_first, jnp.where(in_second, h_second, 0.0))
        weight = jnp.where(in_first, share_first, jnp.where(in_second, share_second, 0.0))
        out = jnp.dot(h.astype(jnp.bfloat16), held[e], preferred_element_type=jnp.float32)
        total_ref[...] += weight * out

    if last:
        keep_ref[...] = total_ref[: rows // 2]
        send_ref[...] = total_ref[rows // 2 :].astype(send_ref.dtype)
    else:
        for copy in copies:
            copy.wait()


def down(x, near, far, hidden, w_down, mine, other, begin, count, before=None):
    experts, half, width = w_down.shape[0], w_down.shape[1] // 2, w_down.shape[2]
    rows = x.shape[0]
    last = before is not None
    operands = [x, near, far, hidden, w_down] + ([other, before] if last else [mine, other])
    part = jax.ShapeDtypeStruct((rows // 2 if last else rows, width), jnp.float32)
    sums = [part, jax.ShapeDtypeStruct(part.shape, jnp.bfloat16)] if last else [part]
    sems = pltpu.SemaphoreType.DMA((count,))
    return pl.pallas_call(
        functools.partial(down_kernel, last, begin, count),
        out_shape=tuple(sums + [pltpu.VMEM(other.shape, other.dtype)]),
        in_specs=[VMEM] * 4 + [HBM] + [VMEM] * 2,
        out_specs=tuple([VMEM] * (len(sums) + 1)),
        input_output_aliases={5 if last else 6: len(sums)},
        scratch_shapes=([pltpu.VMEM((rows, width), jnp.float32)] if last else []) + [sems],
        compiler_params=pltpu.CompilerParams(vmem_limit_bytes=4 * MIB),
        cost_estimate=cost(2 * rows * experts * width * half, 2 * count * width * half),
        name="down_last" if last else "down_mine",
    )(*operands)


def body(tokens, expert_ids, router, w_gate, w_up, w_down):
    bits = steps_of(lax.axis_size("dp"))
    local, width = tokens.shape
    experts = w_gate.shape[0]
    w_gate, w_up, w_down = (
        pltpu.with_memory_space_constraint(w, pltpu.HBM) for w in (w_gate, w_up, w_down)
    )
    early = min(WINDOWS, len(bits))
    ring = None
    for i in range(early):
        ring = load_first(i, w_gate, w_up, ring)
    x = pack(tokens, expert_ids)
    for bit in reversed(bits):
        x = jnp.concatenate([x, swap(x, "dp", bit)], axis=0)
        x = lax.optimization_barrier(x)
    logits = jnp.dot(x[:, :width], router, preferred_element_type=jnp.float32)
    logits = logits + swap(logits, "seq", 1)
    other, ring = gate_up(False, x, w_gate, w_up, ring, early, AHEAD)
    arrived = swap(other, "seq", 1)
    mine, _ = gate_up(True, x, w_gate, w_up, ring, AHEAD, 0)
    pair = mine + arrived
    sent = pair.astype(jnp.bfloat16)
    down_mine, down_other = load_down(w_down, 1)
    far_logits = swap(logits, "seq", 2)
    hidden = hidden_of(pair, swap(sent, "seq", 2))
    hidden_other = swap(hidden, "seq", 1)
    middle = 1 + (experts - 1) // 2
    part, down_other = down(
        x, logits, far_logits, hidden, w_down, down_mine, down_other, 1, middle - 1
    )
    total, send, _ = down(
        x, logits, far_logits, hidden_other, w_down, None, down_other, middle, experts - middle, part
    )
    for bit in bits:
        total = total + swap(send, "dp", bit).astype(jnp.float32)
        if total.shape[0] > local:
            rows = total.shape[0] // 2
            total, send = total[:rows], total[rows:]
    return total.astype(jnp.bfloat16)


def solution(mesh):
    placed = (
        P("dp", "seq"),
        P("dp", None),
        P("seq", None),
        P(None, "seq", "dp"),
        P(None, "seq", "dp"),
        P(None, "dp", "seq"),
    )
    return jax.shard_map(
        body, mesh=mesh, in_specs=placed, out_specs=P("dp", "seq"), check_vma=False
    )
```

```python
import functools

import jax
import jax.numpy as jnp
from jax import lax
from jax.experimental import pallas as pl
from jax.experimental.pallas import tpu as pltpu
from jax.sharding import PartitionSpec as P


LANES = 128
MIB = 1 << 20
WINDOWS = 3
AHEAD = 2
SLOTS = 8
VMEM = pl.BlockSpec(memory_space=pltpu.VMEM)
SMEM = pl.BlockSpec(memory_space=pltpu.SMEM)
HBM = pl.BlockSpec(memory_space=pltpu.HBM)


def steps_of(count):
    return [1 << i for i in range((count - 1).bit_length())]


def swap(value, axis, bit):
    count = lax.axis_size(axis)
    return lax.ppermute(value, axis, [(i, i ^ bit) for i in range(count)])


def cost(flops, moved):
    return pl.CostEstimate(flops=flops, bytes_accessed=moved, transcendentals=0)


def pack_kernel(token_hbm, id_hbm, out_ref, id_ref, sems):
    rows, width = token_hbm.shape
    token_copy = pltpu.make_async_copy(token_hbm, out_ref.at[:, pl.ds(0, width)], sems.at[0])
    id_copy = pltpu.make_async_copy(id_hbm, id_ref, sems.at[1])
    id_copy.start()
    token_copy.start()
    id_copy.wait()
    row = lax.broadcasted_iota(jnp.int32, (rows, rows), 0)
    lane = lax.broadcasted_iota(jnp.int32, (rows, rows), 1)
    place = lax.broadcasted_iota(jnp.int32, (rows, LANES), 1)
    named = jnp.zeros((rows, LANES), jnp.float32)
    for k in range(id_ref.shape[0]):
        numbers = jnp.broadcast_to(id_ref[k : k + 1, :].astype(jnp.float32), (rows, rows))
        column = jnp.sum(jnp.where(row == lane, numbers, 0.0), axis=1, keepdims=True)
        named = jnp.where(place == k, column, named)
    out_ref[:, width:] = named.astype(out_ref.dtype)
    token_copy.wait()


def pack(tokens, expert_ids):
    rows, width = tokens.shape
    return pl.pallas_call(
        pack_kernel,
        out_shape=jax.ShapeDtypeStruct((rows, width + LANES), tokens.dtype),
        in_specs=[HBM, HBM],
        out_specs=VMEM,
        scratch_shapes=[
            pltpu.VMEM(expert_ids.shape[::-1], expert_ids.dtype),
            pltpu.SemaphoreType.DMA((2,)),
        ],
        compiler_params=pltpu.CompilerParams(vmem_limit_bytes=MIB),
        name="pack",
    )(
        pltpu.with_memory_space_constraint(tokens, pltpu.HBM),
        pltpu.with_memory_space_constraint(expert_ids.T, pltpu.HBM),
    )


def block_copy(gate_hbm, up_hbm, number, kind, ring, sems):
    total, half = 2 * gate_hbm.shape[0], gate_hbm.shape[2] // 2
    core = lax.rem(lax.axis_index("seq"), 2)
    if isinstance(number, int):
        side, place, slot = number // total, number % total, number % ring.shape[0]
    else:
        side, place, slot = number // total, lax.rem(number, total), lax.rem(number, ring.shape[0])
    start = pl.multiple_of((core + 1 - side) % 2 * half, half)
    source = gate_hbm if kind == 0 else up_hbm
    return pltpu.make_async_copy(
        source.at[place // 2, :, pl.ds(start, half)], ring.at[slot], sems.at[slot]
    )


def start_block(gate_hbm, up_hbm, number, ring, sems):
    if isinstance(number, int):
        block_copy(gate_hbm, up_hbm, number, number % 2, ring, sems).start()
        return
    for kind in range(2):

        @pl.when(lax.rem(number, 2) == kind)
        def _():
            block_copy(gate_hbm, up_hbm, number, kind, ring, sems).start()


def load_first_kernel(number, gate_hbm, up_hbm, *refs):
    ring, sems = refs[-2:]
    start_block(gate_hbm, up_hbm, number, ring, sems)
    block_copy(gate_hbm, up_hbm, number, 0, ring, sems).wait()


def load_first(number, w_gate, w_up, ring):
    width, half = w_gate.shape[1], w_gate.shape[2] // 2
    slots = min(SLOTS, 2 * w_gate.shape[0])
    return pl.pallas_call(
        functools.partial(load_first_kernel, number),
        out_shape=pltpu.VMEM((slots, width, half), w_gate.dtype),
        in_specs=[HBM, HBM] + ([] if ring is None else [VMEM]),
        out_specs=VMEM,
        input_output_aliases={} if ring is None else {2: 0},
        scratch_shapes=[pltpu.SemaphoreType.DMA((slots,))],
        compiler_params=pltpu.CompilerParams(vmem_limit_bytes=MIB),
        cost_estimate=cost(0, 2 * width * half),
    )(w_gate, w_up, *([] if ring is None else [ring]))


def gate_up_kernel(begin, held, ahead, x_ref, gate_hbm, up_hbm, _, *refs):
    out_ref, ring, sems = refs[-3:]
    experts, width, _ = gate_hbm.shape
    total, slots = 2 * experts, ring.shape[0]
    stop = begin + total + ahead
    x = x_ref[:, :width]
    first = x_ref[:, width : width + 1].astype(jnp.float32)
    second = x_ref[:, width + 1 : width + 2].astype(jnp.float32)
    for number in range(begin + held, min(begin + slots - 1, stop)):
        start_block(gate_hbm, up_hbm, number, ring, sems)
    out_ref[...] = jnp.zeros_like(out_ref)
    half = ring.shape[2]
    if len(refs) > 3:
        router_ref = refs[0]
        out_ref[0, 0, :, half : half + router_ref.shape[0]] = lax.dot_general(
            x, router_ref[...], (((1,), (1,)), ((), ())), preferred_element_type=jnp.float32
        )

    @pl.loop(begin, begin + total)
    def _(number):
        @pl.when(number >= begin + held)
        def _():
            block_copy(gate_hbm, up_hbm, number, 0, ring, sems).wait()

        later = number + slots - 1

        @pl.when(later < stop)
        def _():
            start_block(gate_hbm, up_hbm, later, ring, sems)

        weights = ring[lax.rem(number, slots)]
        value = jnp.dot(x, weights, preferred_element_type=jnp.float32)
        kind, this = lax.rem(number, 2), ((number - begin) // 2).astype(jnp.float32)
        for k, named in ((0, first), (1, second)):
            old = out_ref[kind, k, :, :half]
            out_ref[kind, k, :, :half] = jnp.where(named == this, value, old)

    for number in range(begin + total, stop):
        block_copy(gate_hbm, up_hbm, number, 0, ring, sems).wait()


def gate_up(mine, x, w_gate, w_up, ring, held, ahead, router=None):
    experts, width, columns = w_gate.shape
    rows, half = x.shape[0], columns // 2
    slots = ring.shape[0]
    assert held < slots and ahead < slots
    return pl.pallas_call(
        functools.partial(gate_up_kernel, 2 * experts if mine else 0, held, ahead),
        out_shape=(
            jax.ShapeDtypeStruct((2, 2, rows, half + (0 if mine else LANES)), jnp.float32),
            pltpu.VMEM(ring.shape, ring.dtype),
        ),
        in_specs=[VMEM, HBM, HBM, VMEM] + ([] if mine else [VMEM]),
        out_specs=(VMEM, VMEM),
        input_output_aliases={3: 1},
        scratch_shapes=[pltpu.SemaphoreType.DMA((slots,))],
        compiler_params=pltpu.CompilerParams(vmem_limit_bytes=4 * MIB),
        cost_estimate=cost(
            4 * rows * experts * width * half, 2 * (2 * experts - held + ahead) * width * half
        ),
        name="gate_up_mine" if mine else "gate_up_other",
    )(x, w_gate, w_up, ring, *([] if mine else [router.T]))


def hidden_kernel(pair_ref, far_ref, out_ref):
    gate = pair_ref[0] + far_ref[0].astype(jnp.float32)
    up = pair_ref[1] + far_ref[1].astype(jnp.float32)
    out_ref[...] = (gate / (1.0 + jnp.exp(-gate)) * up).astype(out_ref.dtype)


def hidden_of(pair, far):
    return pl.pallas_call(
        hidden_kernel,
        out_shape=jax.ShapeDtypeStruct(pair.shape[1:], far.dtype),
        in_specs=[VMEM, VMEM],
        out_specs=VMEM,
        compiler_params=pltpu.CompilerParams(vmem_limit_bytes=6 * MIB),
        cost_estimate=pl.CostEstimate(
            flops=8 * pair.size, bytes_accessed=6 * pair.size, transcendentals=pair.size // 2
        ),
        name="silu_times_up",
    )(pair, far)


def piece_copy(mine, down_hbm, expert, held, sem):
    half = down_hbm.shape[1] // 2
    core = lax.rem(lax.axis_index("seq"), 2)
    start = pl.multiple_of((core if mine else 1 - core) * half, half)
    return pltpu.make_async_copy(down_hbm.at[expert, pl.ds(start, half), :], held.at[expert], sem)


def load_down_kernel(count, down_hbm, mine_ref, other_ref, sems):
    experts = down_hbm.shape[0]
    copies = [piece_copy(True, down_hbm, e, mine_ref, sems.at[e]) for e in range(experts)]
    for e in range(count):
        copies.append(piece_copy(False, down_hbm, e, other_ref, sems.at[experts + e]))
    for copy in copies:
        copy.start()
    for copy in copies:
        copy.wait()


def load_down(w_down, count):
    experts, half, width = w_down.shape[0], w_down.shape[1] // 2, w_down.shape[2]
    side = pltpu.VMEM((experts, half, width), w_down.dtype)
    return pl.pallas_call(
        functools.partial(load_down_kernel, count),
        out_shape=(side, side),
        in_specs=[HBM],
        out_specs=(VMEM, VMEM),
        scratch_shapes=[pltpu.SemaphoreType.DMA((2 * experts,))],
        compiler_params=pltpu.CompilerParams(vmem_limit_bytes=MIB),
        cost_estimate=cost(0, 2 * (experts + count) * half * width),
        name="load_down",
    )(w_down)


def down_kernel(last, begin, count, x_ref, near_ref, far_ref, hidden_ref, down_hbm, *refs):
    if last:
        _, before_ref, keep_ref, send_ref, other_ref, total_ref, sems = refs
        held = other_ref
    else:
        held, _, total_ref, other_ref, sems = refs
    copies = [
        piece_copy(False, down_hbm, begin + i, other_ref, sems.at[i]) for i in range(count)
    ]
    for copy in copies:
        copy.start()
    experts, _, width = down_hbm.shape
    rows = x_ref.shape[0]
    first = x_ref[:, width : width + 1].astype(jnp.float32)
    second = x_ref[:, width + 1 : width + 2].astype(jnp.float32)
    logits = near_ref[...] + far_ref[...]
    number = lax.broadcasted_iota(jnp.int32, logits.shape, 1).astype(jnp.float32)
    a = jnp.sum(jnp.where(number == first, logits, 0.0), axis=1, keepdims=True)
    b = jnp.sum(jnp.where(number == second, logits, 0.0), axis=1, keepdims=True)
    share_first = 1.0 / (1.0 + jnp.exp(b - a))
    share_second = 1.0 / (1.0 + jnp.exp(a - b))
    total_ref[...] = before_ref[...] if last else jnp.zeros_like(total_ref)
    h_first = hidden_ref[0].astype(jnp.float32)
    h_second = hidden_ref[1].astype(jnp.float32)

    @pl.loop(0, experts)
    def _(e):
        if last:
            for i in range(count):
                pl.when(e == begin + i)(copies[i].wait)
        this = e.astype(jnp.float32)
        in_first, in_second = first == this, second == this
        h = jnp.where(in_first, h_first, jnp.where(in_second, h_second, 0.0))
        weight = jnp.where(in_first, share_first, jnp.where(in_second, share_second, 0.0))
        out = jnp.dot(h.astype(jnp.bfloat16), held[e], preferred_element_type=jnp.float32)
        total_ref[...] += weight * out

    if last:
        keep_ref[...] = total_ref[: rows // 2]
        send_ref[...] = total_ref[rows // 2 :].astype(send_ref.dtype)
    else:
        for copy in copies:
            copy.wait()


def down(x, near, far, hidden, w_down, mine, other, begin, count, before=None):
    experts, half, width = w_down.shape[0], w_down.shape[1] // 2, w_down.shape[2]
    rows = x.shape[0]
    last = before is not None
    operands = [x, near, far, hidden, w_down] + ([other, before] if last else [mine, other])
    part = jax.ShapeDtypeStruct((rows // 2 if last else rows, width), jnp.float32)
    sums = [part, jax.ShapeDtypeStruct(part.shape, jnp.bfloat16)] if last else [part]
    sems = pltpu.SemaphoreType.DMA((count,))
    return pl.pallas_call(
        functools.partial(down_kernel, last, begin, count),
        out_shape=tuple(sums + [pltpu.VMEM(other.shape, other.dtype)]),
        in_specs=[VMEM] * 4 + [HBM] + [VMEM] * 2,
        out_specs=tuple([VMEM] * (len(sums) + 1)),
        input_output_aliases={5 if last else 6: len(sums)},
        scratch_shapes=([pltpu.VMEM((rows, width), jnp.float32)] if last else []) + [sems],
        compiler_params=pltpu.CompilerParams(vmem_limit_bytes=4 * MIB),
        cost_estimate=cost(2 * rows * experts * width * half, 2 * count * width * half),
        name="down_last" if last else "down_mine",
    )(*operands)


def body(tokens, expert_ids, router, w_gate, w_up, w_down):
    bits = steps_of(lax.axis_size("dp"))
    local = tokens.shape[0]
    experts = w_gate.shape[0]
    w_gate, w_up, w_down = (
        pltpu.with_memory_space_constraint(w, pltpu.HBM) for w in (w_gate, w_up, w_down)
    )
    early = min(WINDOWS, len(bits))
    ring = None
    for i in range(early):
        ring = load_first(i, w_gate, w_up, ring)
    x = pack(tokens, expert_ids)
    for bit in reversed(bits):
        x = jnp.concatenate([x, swap(x, "dp", bit)], axis=0)
        x = lax.optimization_barrier(x)
    other, ring = gate_up(False, x, w_gate, w_up, ring, early, AHEAD, router)
    arrived = swap(other, "seq", 1)
    mine, _ = gate_up(True, x, w_gate, w_up, ring, AHEAD, 0)
    half, stop = mine.shape[-1], mine.shape[-1] + router.shape[1]
    pair = mine + arrived[..., :half]
    logits = other[0, 0, :, half:stop] + arrived[0, 0, :, half:stop]
    sent = pair.astype(jnp.bfloat16)
    down_mine, down_other = load_down(w_down, 1)
    far_logits = swap(logits, "seq", 2)
    hidden = hidden_of(pair, swap(sent, "seq", 2))
    hidden_other = swap(hidden, "seq", 1)
    middle = 1 + (experts - 1) // 2
    part, down_other = down(
        x, logits, far_logits, hidden, w_down, down_mine, down_other, 1, middle - 1
    )
    total, send, _ = down(
        x, logits, far_logits, hidden_other, w_down, None, down_other, middle, experts - middle, part
    )
    for bit in bits:
        total = total + swap(send, "dp", bit).astype(jnp.float32)
        if total.shape[0] > local:
            rows = total.shape[0] // 2
            total, send = total[:rows], total[rows:].astype(jnp.bfloat16)
    return total.astype(jnp.bfloat16)


def solution(mesh):
    placed = (
        P("dp", "seq"),
        P("dp", None),
        P("seq", None),
        P(None, "seq", "dp"),
        P(None, "seq", "dp"),
        P(None, "dp", "seq"),
    )
    return jax.shard_map(
        body, mesh=mesh, in_specs=placed, out_specs=P("dp", "seq"), check_vma=False
    )
```

```python
import functools

import jax
import jax.numpy as jnp
from jax import lax
from jax.experimental import pallas as pl
from jax.experimental.pallas import tpu as pltpu
from jax.sharding import PartitionSpec as P


LANES = 128
MIB = 1 << 20
BESIDE = (1, 2, 2)
AHEAD = 2
SLOTS = 8
VMEM = pl.BlockSpec(memory_space=pltpu.VMEM)
SMEM = pl.BlockSpec(memory_space=pltpu.SMEM)
HBM = pl.BlockSpec(memory_space=pltpu.HBM)


def steps_of(count):
    return [1 << i for i in range((count - 1).bit_length())]


def swap(value, axis, bit):
    count = lax.axis_size(axis)
    return lax.ppermute(value, axis, [(i, i ^ bit) for i in range(count)])


def cost(flops, moved):
    return pl.CostEstimate(flops=flops, bytes_accessed=moved, transcendentals=0)


def pack_kernel(token_hbm, id_hbm, out_ref, id_ref, sems):
    rows, width = token_hbm.shape
    token_copy = pltpu.make_async_copy(token_hbm, out_ref.at[:, pl.ds(0, width)], sems.at[0])
    id_copy = pltpu.make_async_copy(id_hbm, id_ref, sems.at[1])
    id_copy.start()
    token_copy.start()
    id_copy.wait()
    row = lax.broadcasted_iota(jnp.int32, (rows, rows), 0)
    lane = lax.broadcasted_iota(jnp.int32, (rows, rows), 1)
    place = lax.broadcasted_iota(jnp.int32, (rows, LANES), 1)
    named = jnp.zeros((rows, LANES), jnp.float32)
    for k in range(id_ref.shape[0]):
        numbers = jnp.broadcast_to(id_ref[k : k + 1, :].astype(jnp.float32), (rows, rows))
        column = jnp.sum(jnp.where(row == lane, numbers, 0.0), axis=1, keepdims=True)
        named = jnp.where(place == k, column, named)
    out_ref[:, width:] = named.astype(out_ref.dtype)
    token_copy.wait()


def pack(tokens, expert_ids):
    rows, width = tokens.shape
    return pl.pallas_call(
        pack_kernel,
        out_shape=jax.ShapeDtypeStruct((rows, width + LANES), tokens.dtype),
        in_specs=[HBM, HBM],
        out_specs=VMEM,
        scratch_shapes=[
            pltpu.VMEM(expert_ids.shape[::-1], expert_ids.dtype),
            pltpu.SemaphoreType.DMA((2,)),
        ],
        compiler_params=pltpu.CompilerParams(vmem_limit_bytes=MIB),
        name="pack",
    )(
        pltpu.with_memory_space_constraint(tokens, pltpu.HBM),
        pltpu.with_memory_space_constraint(expert_ids.T, pltpu.HBM),
    )


def block_copy(gate_hbm, up_hbm, number, kind, ring, sems):
    total, half = 2 * gate_hbm.shape[0], gate_hbm.shape[2] // 2
    core = lax.rem(lax.axis_index("seq"), 2)
    if isinstance(number, int):
        side, place, slot = number // total, number % total, number % ring.shape[0]
    else:
        side, place, slot = number // total, lax.rem(number, total), lax.rem(number, ring.shape[0])
    start = pl.multiple_of((core + 1 - side) % 2 * half, half)
    source = gate_hbm if kind == 0 else up_hbm
    return pltpu.make_async_copy(
        source.at[place // 2, :, pl.ds(start, half)], ring.at[slot], sems.at[slot]
    )


def start_block(gate_hbm, up_hbm, number, ring, sems):
    if isinstance(number, int):
        block_copy(gate_hbm, up_hbm, number, number % 2, ring, sems).start()
        return
    for kind in range(2):

        @pl.when(lax.rem(number, 2) == kind)
        def _():
            block_copy(gate_hbm, up_hbm, number, kind, ring, sems).start()


def load_first_kernel(begin, stop, gate_hbm, up_hbm, *refs):
    ring, sems = refs[-2:]
    for number in range(begin, stop):
        start_block(gate_hbm, up_hbm, number, ring, sems)
    for number in range(begin, stop):
        block_copy(gate_hbm, up_hbm, number, 0, ring, sems).wait()


def load_first(begin, stop, w_gate, w_up, ring):
    width, half = w_gate.shape[1], w_gate.shape[2] // 2
    slots = min(SLOTS, 2 * w_gate.shape[0])
    return pl.pallas_call(
        functools.partial(load_first_kernel, begin, stop),
        out_shape=pltpu.VMEM((slots, width, half), w_gate.dtype),
        in_specs=[HBM, HBM] + ([] if ring is None else [VMEM]),
        out_specs=VMEM,
        input_output_aliases={} if ring is None else {2: 0},
        scratch_shapes=[pltpu.SemaphoreType.DMA((slots,))],
        compiler_params=pltpu.CompilerParams(vmem_limit_bytes=MIB),
        cost_estimate=cost(0, 2 * (stop - begin) * width * half),
    )(w_gate, w_up, *([] if ring is None else [ring]))


def gate_up_kernel(begin, held, ahead, x_ref, gate_hbm, up_hbm, _, *refs):
    out_ref, ring, sems = refs[-3:]
    experts, width, _ = gate_hbm.shape
    total, slots = 2 * experts, ring.shape[0]
    stop = begin + total + ahead
    x = x_ref[:, :width]
    first = x_ref[:, width : width + 1].astype(jnp.float32)
    second = x_ref[:, width + 1 : width + 2].astype(jnp.float32)
    for number in range(begin + held, min(begin + slots - 1, stop)):
        start_block(gate_hbm, up_hbm, number, ring, sems)
    out_ref[...] = jnp.zeros_like(out_ref)
    half = ring.shape[2]
    if len(refs) > 3:
        router_ref = refs[0]
        out_ref[0, 0, :, half : half + router_ref.shape[0]] = lax.dot_general(
            x, router_ref[...], (((1,), (1,)), ((), ())), preferred_element_type=jnp.float32
        )

    @pl.loop(begin, begin + total)
    def _(number):
        @pl.when(number >= begin + held)
        def _():
            block_copy(gate_hbm, up_hbm, number, 0, ring, sems).wait()

        later = number + slots - 1

        @pl.when(later < stop)
        def _():
            start_block(gate_hbm, up_hbm, later, ring, sems)

        weights = ring[lax.rem(number, slots)]
        value = jnp.dot(x, weights, preferred_element_type=jnp.float32)
        kind, this = lax.rem(number, 2), ((number - begin) // 2).astype(jnp.float32)
        for k, named in ((0, first), (1, second)):
            old = out_ref[kind, k, :, :half]
            out_ref[kind, k, :, :half] = jnp.where(named == this, value, old)

    for number in range(begin + total, stop):
        block_copy(gate_hbm, up_hbm, number, 0, ring, sems).wait()


def gate_up(mine, x, w_gate, w_up, ring, held, ahead, router=None):
    experts, width, columns = w_gate.shape
    rows, half = x.shape[0], columns // 2
    slots = ring.shape[0]
    assert held < slots and ahead < slots
    return pl.pallas_call(
        functools.partial(gate_up_kernel, 2 * experts if mine else 0, held, ahead),
        out_shape=(
            jax.ShapeDtypeStruct((2, 2, rows, half + (0 if mine else LANES)), jnp.float32),
            pltpu.VMEM(ring.shape, ring.dtype),
        ),
        in_specs=[VMEM, HBM, HBM, VMEM] + ([] if mine else [VMEM]),
        out_specs=(VMEM, VMEM),
        input_output_aliases={3: 1},
        scratch_shapes=[pltpu.SemaphoreType.DMA((slots,))],
        compiler_params=pltpu.CompilerParams(vmem_limit_bytes=4 * MIB),
        cost_estimate=cost(
            4 * rows * experts * width * half, 2 * (2 * experts - held + ahead) * width * half
        ),
        name="gate_up_mine" if mine else "gate_up_other",
    )(x, w_gate, w_up, ring, *([] if mine else [router.T]))


def hidden_kernel(pair_ref, far_ref, out_ref):
    gate = pair_ref[0] + far_ref[0].astype(jnp.float32)
    up = pair_ref[1] + far_ref[1].astype(jnp.float32)
    out_ref[...] = (gate / (1.0 + jnp.exp(-gate)) * up).astype(out_ref.dtype)


def hidden_of(pair, far):
    return pl.pallas_call(
        hidden_kernel,
        out_shape=jax.ShapeDtypeStruct(pair.shape[1:], far.dtype),
        in_specs=[VMEM, VMEM],
        out_specs=VMEM,
        compiler_params=pltpu.CompilerParams(vmem_limit_bytes=6 * MIB),
        cost_estimate=pl.CostEstimate(
            flops=8 * pair.size, bytes_accessed=6 * pair.size, transcendentals=pair.size // 2
        ),
        name="silu_times_up",
    )(pair, far)


def piece_copy(mine, down_hbm, expert, held, sem):
    half = down_hbm.shape[1] // 2
    core = lax.rem(lax.axis_index("seq"), 2)
    start = pl.multiple_of((core if mine else 1 - core) * half, half)
    return pltpu.make_async_copy(down_hbm.at[expert, pl.ds(start, half), :], held.at[expert], sem)


def load_down_kernel(count, down_hbm, mine_ref, other_ref, sems):
    experts = down_hbm.shape[0]
    copies = [piece_copy(True, down_hbm, e, mine_ref, sems.at[e]) for e in range(experts)]
    for e in range(count):
        copies.append(piece_copy(False, down_hbm, e, other_ref, sems.at[experts + e]))
    for copy in copies:
        copy.start()
    for copy in copies:
        copy.wait()


def load_down(w_down, count):
    experts, half, width = w_down.shape[0], w_down.shape[1] // 2, w_down.shape[2]
    side = pltpu.VMEM((experts, half, width), w_down.dtype)
    return pl.pallas_call(
        functools.partial(load_down_kernel, count),
        out_shape=(side, side),
        in_specs=[HBM],
        out_specs=(VMEM, VMEM),
        scratch_shapes=[pltpu.SemaphoreType.DMA((2 * experts,))],
        compiler_params=pltpu.CompilerParams(vmem_limit_bytes=MIB),
        cost_estimate=cost(0, 2 * (experts + count) * half * width),
        name="load_down",
    )(w_down)


def down_kernel(last, begin, count, x_ref, near_ref, far_ref, hidden_ref, down_hbm, *refs):
    if last:
        _, before_ref, keep_ref, send_ref, other_ref, total_ref, sems = refs
        held = other_ref
    else:
        held, _, total_ref, other_ref, sems = refs
    copies = [
        piece_copy(False, down_hbm, begin + i, other_ref, sems.at[i]) for i in range(count)
    ]
    for copy in copies:
        copy.start()
    experts, _, width = down_hbm.shape
    rows = x_ref.shape[0]
    first = x_ref[:, width : width + 1].astype(jnp.float32)
    second = x_ref[:, width + 1 : width + 2].astype(jnp.float32)
    logits = near_ref[...] + far_ref[...]
    number = lax.broadcasted_iota(jnp.int32, logits.shape, 1).astype(jnp.float32)
    a = jnp.sum(jnp.where(number == first, logits, 0.0), axis=1, keepdims=True)
    b = jnp.sum(jnp.where(number == second, logits, 0.0), axis=1, keepdims=True)
    share_first = 1.0 / (1.0 + jnp.exp(b - a))
    share_second = 1.0 / (1.0 + jnp.exp(a - b))
    total_ref[...] = before_ref[...] if last else jnp.zeros_like(total_ref)
    h_first = hidden_ref[0].astype(jnp.float32)
    h_second = hidden_ref[1].astype(jnp.float32)

    @pl.loop(0, experts)
    def _(e):
        if last:
            for i in range(count):
                pl.when(e == begin + i)(copies[i].wait)
        this = e.astype(jnp.float32)
        in_first, in_second = first == this, second == this
        h = jnp.where(in_first, h_first, jnp.where(in_second, h_second, 0.0))
        weight = jnp.where(in_first, share_first, jnp.where(in_second, share_second, 0.0))
        out = jnp.dot(h.astype(jnp.bfloat16), held[e], preferred_element_type=jnp.float32)
        total_ref[...] += weight * out

    if last:
        keep_ref[...] = total_ref[: rows // 2]
        send_ref[...] = total_ref[rows // 2 :].astype(send_ref.dtype)
    else:
        for copy in copies:
            copy.wait()


def down(x, near, far, hidden, w_down, mine, other, begin, count, before=None):
    experts, half, width = w_down.shape[0], w_down.shape[1] // 2, w_down.shape[2]
    rows = x.shape[0]
    last = before is not None
    operands = [x, near, far, hidden, w_down] + ([other, before] if last else [mine, other])
    part = jax.ShapeDtypeStruct((rows // 2 if last else rows, width), jnp.float32)
    sums = [part, jax.ShapeDtypeStruct(part.shape, jnp.bfloat16)] if last else [part]
    sems = pltpu.SemaphoreType.DMA((count,))
    return pl.pallas_call(
        functools.partial(down_kernel, last, begin, count),
        out_shape=tuple(sums + [pltpu.VMEM(other.shape, other.dtype)]),
        in_specs=[VMEM] * 4 + [HBM] + [VMEM] * 2,
        out_specs=tuple([VMEM] * (len(sums) + 1)),
        input_output_aliases={5 if last else 6: len(sums)},
        scratch_shapes=([pltpu.VMEM((rows, width), jnp.float32)] if last else []) + [sems],
        compiler_params=pltpu.CompilerParams(vmem_limit_bytes=4 * MIB),
        cost_estimate=cost(2 * rows * experts * width * half, 2 * count * width * half),
        name="down_last" if last else "down_mine",
    )(*operands)


def body(tokens, expert_ids, router, w_gate, w_up, w_down):
    bits = steps_of(lax.axis_size("dp"))
    local = tokens.shape[0]
    experts = w_gate.shape[0]
    w_gate, w_up, w_down = (
        pltpu.with_memory_space_constraint(w, pltpu.HBM) for w in (w_gate, w_up, w_down)
    )
    early, ring = 0, None
    for blocks in BESIDE[: len(bits)]:
        ring = load_first(early, early + blocks, w_gate, w_up, ring)
        early += blocks
    x = pack(tokens, expert_ids)
    for bit in reversed(bits):
        x = jnp.concatenate([x, swap(x, "dp", bit)], axis=0)
        x = lax.optimization_barrier(x)
    other, ring = gate_up(False, x, w_gate, w_up, ring, early, AHEAD, router)
    arrived = swap(other, "seq", 1)
    mine, _ = gate_up(True, x, w_gate, w_up, ring, AHEAD, 0)
    half, stop = mine.shape[-1], mine.shape[-1] + router.shape[1]
    pair = mine + arrived[..., :half]
    logits = other[0, 0, :, half:stop] + arrived[0, 0, :, half:stop]
    sent = pair.astype(jnp.bfloat16)
    down_mine, down_other = load_down(w_down, 1)
    far_logits = swap(logits, "seq", 2)
    hidden = hidden_of(pair, swap(sent, "seq", 2))
    hidden_other = swap(hidden, "seq", 1)
    middle = 1 + (experts - 1) // 2
    part, down_other = down(
        x, logits, far_logits, hidden, w_down, down_mine, down_other, 1, middle - 1
    )
    total, send, _ = down(
        x, logits, far_logits, hidden_other, w_down, None, down_other, middle, experts - middle, part
    )
    for bit in bits:
        total = total + swap(send, "dp", bit).astype(jnp.float32)
        if total.shape[0] > local:
            rows = total.shape[0] // 2
            total, send = total[:rows], total[rows:].astype(jnp.bfloat16)
    return total.astype(jnp.bfloat16)


def solution(mesh):
    placed = (
        P("dp", "seq"),
        P("dp", None),
        P("seq", None),
        P(None, "seq", "dp"),
        P(None, "seq", "dp"),
        P(None, "dp", "seq"),
    )
    return jax.shard_map(
        body, mesh=mesh, in_specs=placed, out_specs=P("dp", "seq"), check_vma=False
    )
```
